32 devices in a mesh: groups: 2 (over x), tm: 8 (over z, y), site: 2 (over core).
Axes of the slice: x: 2, y: 2, z: 4, core: 2. Of those that a mesh axis runs over, the one named last changes fastest.
Arguments:
- features: float32 [4, 4096, 128], P(('groups', 'site'), 'tm'), parts along dimension 0, may hold values from -18 to 18
- forget: float32 [4, 4096, 128], P(('groups', 'site'), 'tm'), parts along dimension 0, may hold values from 1.2207031e-05 to 0.5, as said below
- labels: int32 [4, 4096], P(('groups', 'site'), 'tm'), parts along dimension 0, may hold values from 0 to 127
- lengths: int32 [4], P(('groups', 'site')), parts along dimension 0, may hold values from 2048 to 4096, as said below
- w_conv: bfloat16 [2, 1024, 1024], P(None, ('tm', 'site')), may hold values from -0.1875 to 0.1875
- w_res: bfloat16 [2, 512, 512], P(None, ('tm', 'site')), may hold values from -0.25 to 0.25
- w_in: bfloat16 [128, 512], P(('tm', 'site')), may hold values from -0.5 to 0.5
- w_out: bfloat16 [512, 128], P(('tm', 'site')), may hold values from -0.25 to 0.25
Outputs:
- row_loss: float32 [4, 4096], P(('groups', 'site'), 'tm'), parts along dimension 0
- grad_conv: float32 [4, 1024, 1024], P('groups', ('tm', 'site')), parts along dimension 0
- grad_res: float32 [4, 512, 512], P('groups', ('tm', 'site')), parts along dimension 0
- grad_in: float32 [128, 1024], P(('tm', 'site'), 'groups'), parts along dimension 1
- grad_out: float32 [512, 256], P(('tm', 'site'), 'groups'), parts along dimension 1
The draws below stay inside these ranges and needn't reach their ends.
There are 2 independent parts, one for each index of `groups`. The reference program is written for one: setup_inputs(seed, part) draws one part's arguments, and reference() takes and returns one part's arrays. A program takes and returns all parts, laid end to end along the dimension named above; an argument that names none is the same for every part. Nothing has to cross between parts.
Inputs may be any that keep to these rules, and one draw needn't show every extreme that they name: `forget`: every entry is positive. `lengths`: at least one site is valid over all 4096 steps.
All inputs are finite; a program needn't handle non-finite values.
Results may differ from the reference program's by a relative error of at most 0.02.
Values may be sent and summed in bfloat16 or wider, within the bound.
A program may use at most 128 MiB of HBM per device.

```python
import math
import jax
import jax.numpy as jnp
from jax import lax

C = 512
F = 128
K = 128
LAYERS = 2
BASE_DILATION = 256
T_DEV = 512
SITE_TOTAL = 2
TIME_STEPS = 4096


def draw_features(key, part):
    key_values, key_scales = jax.random.split(key)
    blocks = TIME_STEPS // T_DEV
    raw_values = jnp.clip(jax.random.normal(key_values, (SITE_TOTAL, TIME_STEPS, F), jnp.float32), -6.0, 6.0)
    scales = jnp.exp(jax.random.uniform(key_scales, (SITE_TOTAL, blocks, 1, F), jnp.float32, math.log(0.3), math.log(3.0)))
    return (raw_values.reshape(SITE_TOTAL, blocks, T_DEV, F) * scales).reshape(SITE_TOTAL, TIME_STEPS, F)


def draw_forget(key, part):
    random_subkeys = jax.random.split(key, 6)
    blocks = TIME_STEPS // T_DEV
    share_slow = 0.5
    slow_mask = jax.random.bernoulli(random_subkeys[0], share_slow, (SITE_TOTAL, 1, 1, F))
    fast_rate = jnp.exp(jax.random.uniform(random_subkeys[1], (SITE_TOTAL, 1, 1, F), jnp.float32, math.log(10.0), math.log(17.0))) / T_DEV
    slow_rate = jnp.exp(jax.random.uniform(random_subkeys[2], (SITE_TOTAL, 1, 1, F), jnp.float32, math.log(0.1), math.log(1.0))) / TIME_STEPS
    factors = jnp.exp(jax.random.uniform(random_subkeys[3], (SITE_TOTAL, blocks, 1, F), jnp.float32, math.log(0.5), math.log(2.0)))
    decay_rates = jnp.minimum(jnp.where(slow_mask, slow_rate, fast_rate) * factors, 0.5)
    decay_rates = jnp.broadcast_to(decay_rates, (SITE_TOTAL, blocks, T_DEV, F)).reshape(SITE_TOTAL, TIME_STEPS, F)
    spike_start = jax.random.randint(random_subkeys[4], (SITE_TOTAL, 2), 0, TIME_STEPS)
    spike_active = jnp.any(jnp.arange(TIME_STEPS)[None, :, None] == spike_start[:, None, :], axis=2)
    spike_length = jax.random.uniform(random_subkeys[5], (SITE_TOTAL, TIME_STEPS, 1), jnp.float32, 0.2, 0.5)
    return jnp.where(spike_active[:, :, None], spike_length, decay_rates)


def draw_lengths(key, part):
    key_base = jax.random.fold_in(key, 11)
    key_pick = jax.random.fold_in(key, 12)
    base_lengths = jax.random.randint(key_base, (SITE_TOTAL,), TIME_STEPS // 2, TIME_STEPS + 1)
    chosen_site = jax.random.randint(key_pick, (), 0, SITE_TOTAL)
    return jnp.where(jnp.arange(SITE_TOTAL) == chosen_site, TIME_STEPS, base_lengths).astype(jnp.int32)


def plant(result, key, least, high):
    index_at = [jax.random.randint(jax.random.fold_in(key, axis), (), 0, length) for axis, length in enumerate(result.shape)]
    main_axis = result.shape.index(max(result.shape))
    beside = index_at[:main_axis] + [(index_at[main_axis] + 1) % result.shape[main_axis]] + index_at[main_axis + 1:]
    return result.at[tuple(index_at)].set(least).at[tuple(beside)].set(high)


def block_scale(key, shape, cuts, low, top_value):
    loudness = 1.0
    for position, blocks in cuts:
        draws = jax.random.uniform(jax.random.fold_in(jax.random.fold_in(key, 6), position), (blocks,), jnp.float32, low / len(cuts), top_value / len(cuts))
        loudness = loudness * jnp.repeat(jnp.exp(draws), shape[position] // blocks).reshape((-1,) + (1,) * (len(shape) - 1 - position))
    return loudness


def noise(own_key, shape, deviation, most, cuts=(), held_as=jnp.bfloat16):
    values = deviation * jax.random.normal(own_key, shape, jnp.float32)
    if cuts:
        values = values * block_scale(own_key, shape, cuts, -0.22, 0.18)
    return jnp.clip(values, -most, most).astype(held_as)


def setup_inputs(seed: int = 0, part: int = 0) -> dict:
    key_list = jax.random.split(jax.random.key(seed), 9)
    part_splits = jax.random.split(jax.random.fold_in(key_list[8], part), 9)
    return {
        "features": draw_features(jax.random.fold_in(jax.random.fold_in(key_list[8], part), 71), part),
        "forget": draw_forget(jax.random.fold_in(jax.random.fold_in(key_list[8], part), 71), part),
        "labels": plant(jax.random.randint(part_splits[2], (SITE_TOTAL, TIME_STEPS), 0, K), jax.random.fold_in(part_splits[2], 1), 0, K - 1).astype(jnp.int32),
        "lengths": draw_lengths(jax.random.fold_in(jax.random.fold_in(key_list[8], part), 71), part),
        "w_conv": noise(key_list[4], (LAYERS, 2 * C, 2 * C), (2 * C) ** -0.5, 0.1875, ((1, 16),)),
        "w_res": noise(key_list[5], (LAYERS, C, C), C ** -0.5, 0.25, ((1, 16),)),
        "w_in": noise(key_list[6], (F, C), F ** -0.5, 0.5, ((0, 16),)),
        "w_out": noise(key_list[7], (C, K), C ** -0.5, 0.25, ((0, 16),)),
    }


level_floor = 0.1

def reference(features, forget, labels, lengths, w_conv, w_res, w_in, w_out):
    retain = 1.0 - forget
    inflow = forget * (features * features)

    def advance(carried, inputs):
        mass_sum, weight_sum = carried
        keep_now, inflow_now, forget_now = inputs
        mass_sum = keep_now * mass_sum + inflow_now
        weight_sum = keep_now * weight_sum + forget_now
        return ((mass_sum, weight_sum), mass_sum / weight_sum)
    initial = (jnp.zeros((SITE_TOTAL, F), jnp.float32), jnp.zeros((SITE_TOTAL, F), jnp.float32))
    _, smoothed = lax.scan(advance, initial, (jnp.swapaxes(retain, 0, 1), jnp.swapaxes(inflow, 0, 1), jnp.swapaxes(forget, 0, 1)))
    smoothed = jnp.swapaxes(smoothed, 0, 1)
    normed = (features / jnp.sqrt(smoothed + level_floor)).astype(jnp.bfloat16)
    row_count = SITE_TOTAL * TIME_STEPS
    flat_normed = normed.reshape(row_count, F)
    hidden_now = jnp.dot(flat_normed, w_in, preferred_element_type=jnp.float32).astype(jnp.bfloat16)
    hidden_now = hidden_now.reshape(SITE_TOTAL, TIME_STEPS, C)
    saved_layers = []
    for index_of_layer in range(LAYERS):
        dilation_step = BASE_DILATION * 2 ** index_of_layer
        shifted = jnp.pad(hidden_now, ((0, 0), (dilation_step, 0), (0, 0)))[:, :TIME_STEPS]
        joined = jnp.concatenate([shifted, hidden_now], axis=2).reshape(row_count, 2 * C)
        preact = jnp.dot(joined, w_conv[index_of_layer], preferred_element_type=jnp.float32)
        tanh_part = jnp.tanh(preact[:, :C])
        sigm_part = jax.nn.sigmoid(preact[:, C:])
        gated_out = (tanh_part * sigm_part).astype(jnp.bfloat16)
        updated = hidden_now.reshape(row_count, C).astype(jnp.float32) + jnp.dot(gated_out, w_res[index_of_layer], preferred_element_type=jnp.float32)
        saved_layers.append((joined, tanh_part, sigm_part, gated_out))
        hidden_now = updated.astype(jnp.bfloat16).reshape(SITE_TOTAL, TIME_STEPS, C)
    flat_hidden = hidden_now.reshape(row_count, C)
    logits = jnp.dot(flat_hidden, w_out, preferred_element_type=jnp.float32)
    log_total = jnp.log(lax.optimization_barrier(jnp.sum(jnp.exp(logits), axis=1)))
    target_hot = (labels.reshape(row_count)[:, None] == jnp.arange(K)[None, :]).astype(jnp.float32)
    picked = lax.optimization_barrier(jnp.sum(logits * target_hot, axis=1))
    validity = (jnp.arange(TIME_STEPS)[None, :] < lengths[:, None]).astype(jnp.float32)
    row_loss = (log_total - picked).reshape(SITE_TOTAL, TIME_STEPS) * validity
    loss_scale = 1.0 / math.sqrt(SITE_TOTAL * TIME_STEPS)
    class_probs = jnp.exp(logits - log_total[:, None])
    logit_grad = ((class_probs - target_hot) * (validity.reshape(row_count, 1) * loss_scale)).astype(jnp.bfloat16)
    grad_out = jnp.dot(flat_hidden.T, logit_grad, preferred_element_type=jnp.float32)
    gradient = jnp.dot(logit_grad, w_out.T, preferred_element_type=jnp.float32)
    conv_terms = []
    res_terms = []
    for index_of_layer in reversed(range(LAYERS)):
        dilation_step = BASE_DILATION * 2 ** index_of_layer
        joined, tanh_part, sigm_part, gated_out = saved_layers[index_of_layer]
        rounded = gradient.astype(jnp.bfloat16)
        res_terms.append(jnp.dot(gated_out.T, rounded, preferred_element_type=jnp.float32))
        gated_grad = jnp.dot(rounded, w_res[index_of_layer].T, preferred_element_type=jnp.float32)
        filter_grad = gated_grad * sigm_part * (1.0 - tanh_part * tanh_part)
        gate_grad = gated_grad * tanh_part * sigm_part * (1.0 - sigm_part)
        preact_grad = jnp.concatenate([filter_grad, gate_grad], axis=1).astype(jnp.bfloat16)
        conv_terms.append(jnp.dot(joined.T, preact_grad, preferred_element_type=jnp.float32))
        joined_grad = jnp.dot(preact_grad, w_conv[index_of_layer].T, preferred_element_type=jnp.float32)
        past_grad = joined_grad[:, :C].reshape(SITE_TOTAL, TIME_STEPS, C)
        advanced = jnp.pad(past_grad, ((0, 0), (0, dilation_step), (0, 0)))[:, dilation_step:]
        gradient = gradient + joined_grad[:, C:] + advanced.reshape(row_count, C)
    grad_in = jnp.dot(flat_normed.T, gradient.astype(jnp.bfloat16), preferred_element_type=jnp.float32)
    grad_conv = jnp.stack(conv_terms[::-1])
    grad_res = jnp.stack(res_terms[::-1])
    return (row_loss, grad_conv, grad_res, grad_in, grad_out)
```

```python
import math

import jax
import jax.numpy as jnp
from jax import lax
from jax.sharding import PartitionSpec as P

LAYERS = 2
BASE_DILATION = 256


level_floor = 0.1


def shifted(value, axis, by):
    size = lax.axis_size(axis)
    pairs = [(i, i + by) for i in range(size) if 0 <= i + by < size]
    return lax.ppermute(value, axis, pairs)


def compose(earlier, later):
    retain_first, mass_first, weight_first = earlier
    retain_second, mass_second, weight_second = later
    return (
        retain_first * retain_second,
        retain_second * mass_first + mass_second,
        retain_second * weight_first + weight_second,
    )


def delayed(hidden_now, dilation_step):
    steps_here = hidden_now.shape[1]
    reach_rows = min(dilation_step, steps_here)
    hop_count = -(-dilation_step // steps_here)
    arrived = shifted(hidden_now[:, steps_here - reach_rows :], "tm", hop_count)
    return jnp.concatenate([arrived, hidden_now[:, : steps_here - reach_rows]], axis=1)


def advanced(past_grad, dilation_step):
    steps_here = past_grad.shape[1]
    reach_rows = min(dilation_step, steps_here)
    hop_count = -(-dilation_step // steps_here)
    arrived = shifted(past_grad[:, :reach_rows].astype(jnp.bfloat16), "tm", -hop_count).astype(
        jnp.float32
    )
    return jnp.concatenate([past_grad[:, reach_rows:], arrived], axis=1)


def gather_weights(*weights):
    shard_devices = lax.axis_size("tm") * lax.axis_size("site")
    flat = jnp.concatenate([w.reshape(-1) for w in weights])
    stacked = lax.all_gather(flat, ("tm", "site"), axis=0, tiled=False)
    full = []
    start = 0
    for w in weights:
        size = w.size
        piece = stacked[:, start : start + size]
        start += size
        if w.ndim == 3:
            piece = piece.reshape(shard_devices, w.shape[0], w.shape[1], w.shape[2])
            piece = piece.transpose(1, 0, 2, 3).reshape(
                w.shape[0], shard_devices * w.shape[1], w.shape[2]
            )
        else:
            piece = piece.reshape(shard_devices * w.shape[0], w.shape[1])
        full.append(piece)
    return full


def scatter_terms(*terms):
    shard_devices = lax.axis_size("tm") * lax.axis_size("site")
    flat = []
    for t in terms:
        if t.ndim == 3:
            piece = t.reshape(t.shape[0], shard_devices, t.shape[1] // shard_devices, t.shape[2])
            piece = piece.transpose(1, 0, 2, 3)
        else:
            piece = t
        flat.append(piece.reshape(shard_devices, -1).astype(jnp.bfloat16))
    joined_terms = jnp.concatenate(flat, axis=1)
    reduced = lax.psum_scatter(
        joined_terms.reshape(shard_devices * 64, -1), ("tm", "site"), scatter_dimension=0, tiled=True
    ).astype(jnp.float32).reshape(-1)
    out = []
    start = 0
    for t in terms:
        size = t.size // shard_devices
        piece = reduced[start : start + size]
        start += size
        if t.ndim == 3:
            piece = piece.reshape(t.shape[0], t.shape[1] // shard_devices, t.shape[2])
        else:
            piece = piece.reshape(t.shape[0] // shard_devices, t.shape[1])
        out.append(piece)
    return out


def on_device(features, forget, labels, lengths, w_conv, w_res, w_in, w_out):
    site_count, steps_here, band_count = features.shape
    row_count = site_count * steps_here
    time_devices = lax.axis_size("tm")
    site_devices = lax.axis_size("site")
    retain = 1.0 - forget
    inflow = forget * (features * features)
    within = lax.associative_scan(compose, (retain, inflow, forget), axis=1)
    summary = (within[0][:, -1], within[1][:, -1], within[2][:, -1])
    identity = (jnp.ones_like(summary[0]), jnp.zeros_like(summary[1]), jnp.zeros_like(summary[2]))
    packed = lax.all_gather(jnp.stack(summary), "tm", axis=0, tiled=False)
    shaped = tuple(packed[:, index] for index in range(3))
    inclusive = lax.associative_scan(compose, shaped, axis=0)
    position = lax.axis_index("tm")
    before = jnp.maximum(position - 1, 0)
    carried = tuple(
        (
            jnp.where(
                position > 0, lax.dynamic_index_in_dim(member, before, 0, keepdims=False), neutral
            )
            for member, neutral in zip(inclusive, identity)
        )
    )
    mass_sum = within[0] * carried[1][:, None, :] + within[1]
    weight_sum = within[0] * carried[2][:, None, :] + within[2]
    smoothed = mass_sum / weight_sum
    normed = (features / jnp.sqrt(smoothed + level_floor)).astype(jnp.bfloat16)
    flat_normed = normed.reshape(row_count, band_count)
    conv_all, res_all, in_all, out_all = gather_weights(w_conv, w_res, w_in, w_out)
    channels = res_all.shape[1]
    hidden_now = jnp.dot(flat_normed, in_all, preferred_element_type=jnp.float32).astype(
        jnp.bfloat16
    )
    hidden_now = hidden_now.reshape(site_count, steps_here, channels)
    saved_layers = []
    for index_of_layer in range(LAYERS):
        dilation_step = BASE_DILATION * 2**index_of_layer
        joined = jnp.concatenate([delayed(hidden_now, dilation_step), hidden_now], axis=2).reshape(
            row_count, 2 * channels
        )
        preact = jnp.dot(joined, conv_all[index_of_layer], preferred_element_type=jnp.float32)
        tanh_part = jnp.tanh(preact[:, :channels])
        sigm_part = jax.nn.sigmoid(preact[:, channels:])
        gated_out = (tanh_part * sigm_part).astype(jnp.bfloat16)
        updated = hidden_now.reshape(row_count, channels).astype(jnp.float32) + jnp.dot(
            gated_out, res_all[index_of_layer], preferred_element_type=jnp.float32
        )
        saved_layers.append((joined, tanh_part, sigm_part, gated_out))
        hidden_now = updated.astype(jnp.bfloat16).reshape(site_count, steps_here, channels)
    flat_hidden = hidden_now.reshape(row_count, channels)
    logits = jnp.dot(flat_hidden, out_all, preferred_element_type=jnp.float32)
    classes = logits.shape[1]
    log_total = jnp.log(jnp.sum(jnp.exp(logits), axis=1))
    target_hot = (labels.reshape(row_count)[:, None] == jnp.arange(classes)[None, :]).astype(
        jnp.float32
    )
    picked = jnp.sum(logits * target_hot, axis=1)
    positions = lax.axis_index("tm") * steps_here + jnp.arange(steps_here)
    validity = (positions[None, :] < lengths[:, None]).astype(jnp.float32)
    row_loss = (log_total - picked).reshape(site_count, steps_here) * validity
    loss_scale = 1.0 / math.sqrt(site_count * site_devices * steps_here * time_devices)
    class_probs = jnp.exp(logits - log_total[:, None])
    logit_grad = (
        (class_probs - target_hot) * (validity.reshape(row_count, 1) * loss_scale)
    ).astype(jnp.bfloat16)
    term_out = jnp.dot(flat_hidden.T, logit_grad, preferred_element_type=jnp.float32)
    gradient = jnp.dot(logit_grad, out_all.T, preferred_element_type=jnp.float32)
    conv_terms = []
    res_terms = []
    for index_of_layer in reversed(range(LAYERS)):
        dilation_step = BASE_DILATION * 2**index_of_layer
        joined, tanh_part, sigm_part, gated_out = saved_layers[index_of_layer]
        rounded = gradient.astype(jnp.bfloat16)
        res_terms.append(jnp.dot(gated_out.T, rounded, preferred_element_type=jnp.float32))
        gated_grad = jnp.dot(rounded, res_all[index_of_layer].T, preferred_element_type=jnp.float32)
        filter_grad = gated_grad * sigm_part * (1.0 - tanh_part * tanh_part)
        gate_grad = gated_grad * tanh_part * sigm_part * (1.0 - sigm_part)
        preact_grad = jnp.concatenate([filter_grad, gate_grad], axis=1).astype(jnp.bfloat16)
        conv_terms.append(jnp.dot(joined.T, preact_grad, preferred_element_type=jnp.float32))
        joined_grad = jnp.dot(
            preact_grad, conv_all[index_of_layer].T, preferred_element_type=jnp.float32
        )
        past_grad = joined_grad[:, :channels].reshape(site_count, steps_here, channels)
        gradient = (
            gradient
            + joined_grad[:, channels:]
            + advanced(past_grad, dilation_step).reshape(row_count, channels)
        )
    term_in = jnp.dot(
        flat_normed.T, gradient.astype(jnp.bfloat16), preferred_element_type=jnp.float32
    )
    term_conv = jnp.stack(conv_terms[::-1])
    term_res = jnp.stack(res_terms[::-1])
    grad_conv, grad_res, grad_in, grad_out = scatter_terms(term_conv, term_res, term_in, term_out)
    return (row_loss, grad_conv, grad_res, grad_in, grad_out)


def solution(mesh):
    return jax.shard_map(
        on_device,
        mesh=mesh,
        in_specs=(
            P(("groups", "site"), "tm", None),
            P(("groups", "site"), "tm", None),
            P(("groups", "site"), "tm"),
            P(("groups", "site")),
            P(None, ("tm", "site"), None),
            P(None, ("tm", "site"), None),
            P(("tm", "site"), None),
            P(("tm", "site"), None),
        ),
        out_specs=(
            P(("groups", "site"), "tm"),
            P("groups", ("tm", "site"), None),
            P("groups", ("tm", "site"), None),
            P(("tm", "site"), "groups"),
            P(("tm", "site"), "groups"),
        ),
        check_vma=False,
    )
```

```python
import math

import jax
import jax.numpy as jnp
from jax import lax
from jax.sharding import PartitionSpec as P

LAYERS = 2
BASE_DILATION = 256


level_floor = 0.1


def shifted(value, axis, by):
    size = lax.axis_size(axis)
    pairs = [(i, i + by) for i in range(size) if 0 <= i + by < size]
    return lax.ppermute(value, axis, pairs)


def compose(earlier, later):
    retain_first, mass_first, weight_first = earlier
    retain_second, mass_second, weight_second = later
    return (
        retain_first * retain_second,
        retain_second * mass_first + mass_second,
        retain_second * weight_first + weight_second,
    )


def delayed(hidden_now, dilation_step):
    steps_here = hidden_now.shape[1]
    reach_rows = min(dilation_step, steps_here)
    hop_count = -(-dilation_step // steps_here)
    arrived = shifted(hidden_now[:, steps_here - reach_rows :], "tm", hop_count)
    return jnp.concatenate([arrived, hidden_now[:, : steps_here - reach_rows]], axis=1)


def advanced(past_grad, dilation_step):
    steps_here = past_grad.shape[1]
    reach_rows = min(dilation_step, steps_here)
    hop_count = -(-dilation_step // steps_here)
    arrived = shifted(past_grad[:, :reach_rows].astype(jnp.bfloat16), "tm", -hop_count).astype(
        jnp.float32
    )
    return jnp.concatenate([past_grad[:, reach_rows:], arrived], axis=1)


def gather_weights(*weights):
    shard_devices = lax.axis_size("tm") * lax.axis_size("site")
    flat = jnp.concatenate([w.reshape(-1) for w in weights])
    stacked = lax.all_gather(flat, ("tm", "site"), axis=0, tiled=False)
    full = []
    start = 0
    for w in weights:
        size = w.size
        piece = stacked[:, start : start + size]
        start += size
        if w.ndim == 4:
            piece = piece.reshape((shard_devices,) + w.shape)
        elif w.ndim == 3:
            piece = piece.reshape(shard_devices, w.shape[0], w.shape[1], w.shape[2])
            piece = piece.transpose(1, 0, 2, 3).reshape(
                w.shape[0], shard_devices * w.shape[1], w.shape[2]
            )
        else:
            piece = piece.reshape(shard_devices * w.shape[0], w.shape[1])
        full.append(piece)
    return full


def scatter_terms(*terms):
    shard_devices = lax.axis_size("tm") * lax.axis_size("site")
    flat = []
    for t in terms:
        if t.ndim == 3:
            piece = t.reshape(t.shape[0], shard_devices, t.shape[1] // shard_devices, t.shape[2])
            piece = piece.transpose(1, 0, 2, 3)
        else:
            piece = t
        flat.append(piece.reshape(shard_devices, -1).astype(jnp.bfloat16))
    joined_terms = jnp.concatenate(flat, axis=1)
    reduced = lax.psum_scatter(
        joined_terms.reshape(shard_devices * 64, -1), ("tm", "site"), scatter_dimension=0, tiled=True
    ).astype(jnp.float32).reshape(-1)
    out = []
    start = 0
    for t in terms:
        size = t.size // shard_devices
        piece = reduced[start : start + size]
        start += size
        if t.ndim == 3:
            piece = piece.reshape(t.shape[0], t.shape[1] // shard_devices, t.shape[2])
        else:
            piece = piece.reshape(t.shape[0] // shard_devices, t.shape[1])
        out.append(piece)
    return out


def on_device(features, forget, labels, lengths, w_conv, w_res, w_in, w_out):
    site_count, steps_here, band_count = features.shape
    row_count = site_count * steps_here
    time_devices = lax.axis_size("tm")
    site_devices = lax.axis_size("site")
    retain = 1.0 - forget
    inflow = forget * (features * features)
    within = lax.associative_scan(compose, (retain, inflow, forget), axis=1)
    summary = (within[0][:, -1], within[1][:, -1], within[2][:, -1])
    identity = (jnp.ones_like(summary[0]), jnp.zeros_like(summary[1]), jnp.zeros_like(summary[2]))
    summary_rest = jnp.stack(summary)
    summary_parts = []
    for _ in range(3):
        part = summary_rest.astype(jnp.bfloat16)
        summary_parts.append(part)
        summary_rest = summary_rest - part.astype(jnp.float32)
    summary_bits = jnp.stack(summary_parts, axis=-1)
    conv_all, res_all, in_all, out_all, summary_all = gather_weights(
        w_conv, w_res, w_in, w_out, summary_bits
    )
    summary_all = summary_all.astype(jnp.float32)
    summary_all = (summary_all[..., 0] + summary_all[..., 1] + summary_all[..., 2]).reshape(
        time_devices, site_devices, 3, site_count, band_count
    )
    packed = lax.dynamic_index_in_dim(summary_all, lax.axis_index("site"), 1, keepdims=False)
    shaped = tuple(packed[:, index] for index in range(3))
    inclusive = lax.associative_scan(compose, shaped, axis=0)
    position = lax.axis_index("tm")
    before = jnp.maximum(position - 1, 0)
    carried = tuple(
        (
            jnp.where(
                position > 0, lax.dynamic_index_in_dim(member, before, 0, keepdims=False), neutral
            )
            for member, neutral in zip(inclusive, identity)
        )
    )
    mass_sum = within[0] * carried[1][:, None, :] + within[1]
    weight_sum = within[0] * carried[2][:, None, :] + within[2]
    smoothed = mass_sum / weight_sum
    normed = (features / jnp.sqrt(smoothed + level_floor)).astype(jnp.bfloat16)
    flat_normed = normed.reshape(row_count, band_count)
    channels = res_all.shape[1]
    hidden_now = jnp.dot(flat_normed, in_all, preferred_element_type=jnp.float32).astype(
        jnp.bfloat16
    )
    hidden_now = hidden_now.reshape(site_count, steps_here, channels)
    saved_layers = []
    for index_of_layer in range(LAYERS):
        dilation_step = BASE_DILATION * 2**index_of_layer
        joined = jnp.concatenate([delayed(hidden_now, dilation_step), hidden_now], axis=2).reshape(
            row_count, 2 * channels
        )
        preact = jnp.dot(joined, conv_all[index_of_layer], preferred_element_type=jnp.float32)
        tanh_part = jnp.tanh(preact[:, :channels])
        sigm_part = jax.nn.sigmoid(preact[:, channels:])
        gated_out = (tanh_part * sigm_part).astype(jnp.bfloat16)
        updated = hidden_now.reshape(row_count, channels).astype(jnp.float32) + jnp.dot(
            gated_out, res_all[index_of_layer], preferred_element_type=jnp.float32
        )
        saved_layers.append((joined, tanh_part, sigm_part, gated_out))
        hidden_now = updated.astype(jnp.bfloat16).reshape(site_count, steps_here, channels)
    flat_hidden = hidden_now.reshape(row_count, channels)
    logits = jnp.dot(flat_hidden, out_all, preferred_element_type=jnp.float32)
    classes = logits.shape[1]
    log_total = jnp.log(jnp.sum(jnp.exp(logits), axis=1))
    target_hot = (labels.reshape(row_count)[:, None] == jnp.arange(classes)[None, :]).astype(
        jnp.float32
    )
    picked = jnp.sum(logits * target_hot, axis=1)
    positions = lax.axis_index("tm") * steps_here + jnp.arange(steps_here)
    validity = (positions[None, :] < lengths[:, None]).astype(jnp.float32)
    row_loss = (log_total - picked).reshape(site_count, steps_here) * validity
    loss_scale = 1.0 / math.sqrt(site_count * site_devices * steps_here * time_devices)
    class_probs = jnp.exp(logits - log_total[:, None])
    logit_grad = (
        (class_probs - target_hot) * (validity.reshape(row_count, 1) * loss_scale)
    ).astype(jnp.bfloat16)
    term_out = jnp.dot(flat_hidden.T, logit_grad, preferred_element_type=jnp.float32)
    gradient = jnp.dot(logit_grad, out_all.T, preferred_element_type=jnp.float32)
    conv_terms = []
    res_terms = []
    for index_of_layer in reversed(range(LAYERS)):
        dilation_step = BASE_DILATION * 2**index_of_layer
        joined, tanh_part, sigm_part, gated_out = saved_layers[index_of_layer]
        rounded = gradient.astype(jnp.bfloat16)
        res_terms.append(jnp.dot(gated_out.T, rounded, preferred_element_type=jnp.float32))
        gated_grad = jnp.dot(rounded, res_all[index_of_layer].T, preferred_element_type=jnp.float32)
        filter_grad = gated_grad * sigm_part * (1.0 - tanh_part * tanh_part)
        gate_grad = gated_grad * tanh_part * sigm_part * (1.0 - sigm_part)
        preact_grad = jnp.concatenate([filter_grad, gate_grad], axis=1).astype(jnp.bfloat16)
        conv_terms.append(jnp.dot(joined.T, preact_grad, preferred_element_type=jnp.float32))
        joined_grad = jnp.dot(
            preact_grad, conv_all[index_of_layer].T, preferred_element_type=jnp.float32
        )
        past_grad = joined_grad[:, :channels].reshape(site_count, steps_here, channels)
        gradient = (
            gradient
            + joined_grad[:, channels:]
            + advanced(past_grad, dilation_step).reshape(row_count, channels)
        )
    term_in = jnp.dot(
        flat_normed.T, gradient.astype(jnp.bfloat16), preferred_element_type=jnp.float32
    )
    term_conv = jnp.stack(conv_terms[::-1])
    term_res = jnp.stack(res_terms[::-1])
    grad_conv, grad_res, grad_in, grad_out = scatter_terms(term_conv, term_res, term_in, term_out)
    return (row_loss, grad_conv, grad_res, grad_in, grad_out)


def solution(mesh):
    return jax.shard_map(
        on_device,
        mesh=mesh,
        in_specs=(
            P(("groups", "site"), "tm", None),
            P(("groups", "site"), "tm", None),
            P(("groups", "site"), "tm"),
            P(("groups", "site")),
            P(None, ("tm", "site"), None),
            P(None, ("tm", "site"), None),
            P(("tm", "site"), None),
            P(("tm", "site"), None),
        ),
        out_specs=(
            P(("groups", "site"), "tm"),
            P("groups", ("tm", "site"), None),
            P("groups", ("tm", "site"), None),
            P(("tm", "site"), "groups"),
            P(("tm", "site"), "groups"),
        ),
        check_vma=False,
    )
```

```python
import math

import jax
import jax.numpy as jnp
from jax import lax
from jax.sharding import PartitionSpec as P

LAYERS = 2
BASE_DILATION = 256


level_floor = 0.1


def shifted(value, axis, by):
    size = lax.axis_size(axis)
    pairs = [(i, i + by) for i in range(size) if 0 <= i + by < size]
    return lax.ppermute(value, axis, pairs)


def compose(earlier, later):
    retain_first, mass_first, weight_first = earlier
    retain_second, mass_second, weight_second = later
    return (
        retain_first * retain_second,
        retain_second * mass_first + mass_second,
        retain_second * weight_first + weight_second,
    )


def delayed(hidden_now, dilation_step):
    steps_here = hidden_now.shape[1]
    reach_rows = min(dilation_step, steps_here)
    hop_count = -(-dilation_step // steps_here)
    arrived = shifted(hidden_now[:, steps_here - reach_rows :], "tm", hop_count)
    return jnp.concatenate([arrived, hidden_now[:, : steps_here - reach_rows]], axis=1)


def advanced(past_grad, dilation_step):
    steps_here = past_grad.shape[1]
    reach_rows = min(dilation_step, steps_here)
    hop_count = -(-dilation_step // steps_here)
    arrived = shifted(past_grad[:, :reach_rows].astype(jnp.bfloat16), "tm", -hop_count).astype(
        jnp.float32
    )
    return jnp.concatenate([past_grad[:, reach_rows:], arrived], axis=1)


def gather_weights(*weights):
    shard_devices = lax.axis_size("tm") * lax.axis_size("site")
    flat = jnp.concatenate([w.reshape(-1) for w in weights])
    stacked = lax.all_gather(flat, ("tm", "site"), axis=0, tiled=False)
    full = []
    start = 0
    for w in weights:
        size = w.size
        piece = stacked[:, start : start + size]
        start += size
        if w.ndim == 3:
            piece = piece.reshape(shard_devices, w.shape[0], w.shape[1], w.shape[2])
            piece = piece.transpose(1, 0, 2, 3).reshape(
                w.shape[0], shard_devices * w.shape[1], w.shape[2]
            )
        else:
            piece = piece.reshape(shard_devices * w.shape[0], w.shape[1])
        full.append(piece)
    return full


def scatter_terms(*terms):
    shard_devices = lax.axis_size("tm") * lax.axis_size("site")
    flat = []
    for t in terms:
        if t.ndim == 3:
            piece = t.reshape(t.shape[0], shard_devices, t.shape[1] // shard_devices, t.shape[2])
            piece = piece.transpose(1, 0, 2, 3)
        else:
            piece = t
        flat.append(piece.reshape(shard_devices, -1).astype(jnp.bfloat16))
    time_devices = lax.axis_size("tm")
    site_devices = lax.axis_size("site")
    joined_terms = jnp.concatenate(flat, axis=1)
    width = joined_terms.shape[1]
    by_site = joined_terms.reshape(time_devices, site_devices, width).transpose(1, 0, 2)
    site_reduced = lax.psum_scatter(
        by_site.reshape(site_devices * time_devices * 8, -1), "site", scatter_dimension=0, tiled=True
    )
    reduced = lax.psum_scatter(
        site_reduced.reshape(time_devices * 64, -1), "tm", scatter_dimension=0, tiled=True
    ).astype(jnp.float32).reshape(-1)
    out = []
    start = 0
    for t in terms:
        size = t.size // shard_devices
        piece = reduced[start : start + size]
        start += size
        if t.ndim == 3:
            piece = piece.reshape(t.shape[0], t.shape[1] // shard_devices, t.shape[2])
        else:
            piece = piece.reshape(t.shape[0] // shard_devices, t.shape[1])
        out.append(piece)
    return out


def on_device(features, forget, labels, lengths, w_conv, w_res, w_in, w_out):
    site_count, steps_here, band_count = features.shape
    row_count = site_count * steps_here
    time_devices = lax.axis_size("tm")
    site_devices = lax.axis_size("site")
    retain = 1.0 - forget
    inflow = forget * (features * features)
    within = lax.associative_scan(compose, (retain, inflow, forget), axis=1)
    summary = (within[0][:, -1], within[1][:, -1], within[2][:, -1])
    identity = (jnp.ones_like(summary[0]), jnp.zeros_like(summary[1]), jnp.zeros_like(summary[2]))
    packed = lax.all_gather(jnp.stack(summary), "tm", axis=0, tiled=False)
    shaped = tuple(packed[:, index] for index in range(3))
    inclusive = lax.associative_scan(compose, shaped, axis=0)
    position = lax.axis_index("tm")
    before = jnp.maximum(position - 1, 0)
    carried = tuple(
        (
            jnp.where(
                position > 0, lax.dynamic_index_in_dim(member, before, 0, keepdims=False), neutral
            )
            for member, neutral in zip(inclusive, identity)
        )
    )
    mass_sum = within[0] * carried[1][:, None, :] + within[1]
    weight_sum = within[0] * carried[2][:, None, :] + within[2]
    smoothed = mass_sum / weight_sum
    normed = (features / jnp.sqrt(smoothed + level_floor)).astype(jnp.bfloat16)
    flat_normed = normed.reshape(row_count, band_count)
    conv_all, res_all, in_all, out_all = gather_weights(w_conv, w_res, w_in, w_out)
    channels = res_all.shape[1]
    hidden_now = jnp.dot(flat_normed, in_all, preferred_element_type=jnp.float32).astype(
        jnp.bfloat16
    )
    hidden_now = hidden_now.reshape(site_count, steps_here, channels)
    saved_layers = []
    for index_of_layer in range(LAYERS):
        dilation_step = BASE_DILATION * 2**index_of_layer
        joined = jnp.concatenate([delayed(hidden_now, dilation_step), hidden_now], axis=2).reshape(
            row_count, 2 * channels
        )
        preact = jnp.dot(joined, conv_all[index_of_layer], preferred_element_type=jnp.float32)
        tanh_part = jnp.tanh(preact[:, :channels])
        sigm_part = jax.nn.sigmoid(preact[:, channels:])
        gated_out = (tanh_part * sigm_part).astype(jnp.bfloat16)
        updated = hidden_now.reshape(row_count, channels).astype(jnp.float32) + jnp.dot(
            gated_out, res_all[index_of_layer], preferred_element_type=jnp.float32
        )
        saved_layers.append((joined, tanh_part, sigm_part, gated_out))
        hidden_now = updated.astype(jnp.bfloat16).reshape(site_count, steps_here, channels)
    flat_hidden = hidden_now.reshape(row_count, channels)
    logits = jnp.dot(flat_hidden, out_all, preferred_element_type=jnp.float32)
    classes = logits.shape[1]
    log_total = jnp.log(jnp.sum(jnp.exp(logits), axis=1))
    target_hot = (labels.reshape(row_count)[:, None] == jnp.arange(classes)[None, :]).astype(
        jnp.float32
    )
    picked = jnp.sum(logits * target_hot, axis=1)
    positions = lax.axis_index("tm") * steps_here + jnp.arange(steps_here)
    validity = (positions[None, :] < lengths[:, None]).astype(jnp.float32)
    row_loss = (log_total - picked).reshape(site_count, steps_here) * validity
    loss_scale = 1.0 / math.sqrt(site_count * site_devices * steps_here * time_devices)
    class_probs = jnp.exp(logits - log_total[:, None])
    logit_grad = (
        (class_probs - target_hot) * (validity.reshape(row_count, 1) * loss_scale)
    ).astype(jnp.bfloat16)
    term_out = jnp.dot(flat_hidden.T, logit_grad, preferred_element_type=jnp.float32)
    gradient = jnp.dot(logit_grad, out_all.T, preferred_element_type=jnp.float32)
    conv_terms = []
    res_terms = []
    for index_of_layer in reversed(range(LAYERS)):
        dilation_step = BASE_DILATION * 2**index_of_layer
        joined, tanh_part, sigm_part, gated_out = saved_layers[index_of_layer]
        rounded = gradient.astype(jnp.bfloat16)
        res_terms.append(jnp.dot(gated_out.T, rounded, preferred_element_type=jnp.float32))
        gated_grad = jnp.dot(rounded, res_all[index_of_layer].T, preferred_element_type=jnp.float32)
        filter_grad = gated_grad * sigm_part * (1.0 - tanh_part * tanh_part)
        gate_grad = gated_grad * tanh_part * sigm_part * (1.0 - sigm_part)
        preact_grad = jnp.concatenate([filter_grad, gate_grad], axis=1).astype(jnp.bfloat16)
        conv_terms.append(jnp.dot(joined.T, preact_grad, preferred_element_type=jnp.float32))
        joined_grad = jnp.dot(
            preact_grad, conv_all[index_of_layer].T, preferred_element_type=jnp.float32
        )
        past_grad = joined_grad[:, :channels].reshape(site_count, steps_here, channels)
        gradient = (
            gradient
            + joined_grad[:, channels:]
            + advanced(past_grad, dilation_step).reshape(row_count, channels)
        )
    term_in = jnp.dot(
        flat_normed.T, gradient.astype(jnp.bfloat16), preferred_element_type=jnp.float32
    )
    term_conv = jnp.stack(conv_terms[::-1])
    term_res = jnp.stack(res_terms[::-1])
    grad_conv, grad_res, grad_in, grad_out = scatter_terms(term_conv, term_res, term_in, term_out)
    return (row_loss, grad_conv, grad_res, grad_in, grad_out)


def solution(mesh):
    return jax.shard_map(
        on_device,
        mesh=mesh,
        in_specs=(
            P(("groups", "site"), "tm", None),
            P(("groups", "site"), "tm", None),
            P(("groups", "site"), "tm"),
            P(("groups", "site")),
            P(None, ("tm", "site"), None),
            P(None, ("tm", "site"), None),
            P(("tm", "site"), None),
            P(("tm", "site"), None),
        ),
        out_specs=(
            P(("groups", "site"), "tm"),
            P("groups", ("tm", "site"), None),
            P("groups", ("tm", "site"), None),
            P(("tm", "site"), "groups"),
            P(("tm", "site"), "groups"),
        ),
        check_vma=False,
    )
```
